512 devices in a mesh: edge: 8 (over x, core), frame: 64 (over y, z).
Axes of the slice: x: 4, y: 8, z: 8, core: 2. Of those that a mesh axis runs over, the one named last changes fastest.
Arguments:
- inv_depth: float32 [2048, 1280], P('frame'), may hold values from 0.3 to 2
- poses: float32 [6, 2048], P(None, 'frame'), may hold values from -1.2 to 1.2
- targets: int32 [2048, 8], P('frame'), may hold values from 0 to 2047, as said below
- degree: int32 [2048], P('frame'), may hold values from 2 to 8, as said below
- flow: bfloat16 [2048, 8, 2, 1280], P('frame', 'edge'), may hold values from -6 to 6
- confidence: bfloat16 [2048, 8, 1280], P('frame', 'edge'), may hold values from 0.099609375 to 1
- damping_index: int32 [1], replicated, may hold values from 4096 to 4159
- panel_index: int32 [1], replicated, may hold values from 0 to 255
Outputs:
- panel: float32 [12288, 48], P(('edge', 'frame'))
- updated_rhs: float32 [12288], P(('edge', 'frame'))
The draws below stay inside these ranges and needn't reach their ends.
Inputs may be any that keep to these rules, and one draw needn't show every extreme that they name: `targets`: row i names 8 different keyframes, none of them i; every keyframe is named in exactly 8 slots over all rows. Slots 0 to degree - 1 of a keyframe are edges, the others are empty; some keyframe fills all 8.
All inputs are finite; a program needn't handle non-finite values.
Results may differ from the reference program's by a relative error of at most 0.0005.
Values may be sent and summed in bfloat16 or wider, within the bound.
No kernel may reach another device: no remote copies, remote signals or barrier semaphores. Data moves between devices by JAX's collectives and lax.ppermute only.
A program may use at most 64 MiB of HBM per device.

```python
import math
import jax
import jax.numpy as jnp
from jax import lax

COLS = 80
DEG = 8
PANEL_F = 8
PIXELS = 1280
FRAMES = 2048
N_FRAME = 64


def draw_targets(key, part):
    relabel = jax.random.permutation(jax.random.fold_in(key, 11), FRAMES).astype(jnp.int32)
    frame_ids = jnp.arange(FRAMES, dtype=jnp.int32)
    inverse_label = jnp.zeros((FRAMES,), jnp.int32).at[relabel].set(frame_ids)
    scores = jax.random.randint(jax.random.fold_in(key, 12), (FRAMES - 1,), 0, 2 ** 19)
    scores = scores * FRAMES + jnp.arange(FRAMES - 1, dtype=jnp.int32)
    offsets = (lax.top_k(scores, DEG)[1] + 1).astype(jnp.int32)
    shifted = (relabel[:, None] + offsets[None, :]) % FRAMES
    return jnp.take(inverse_label, shifted, axis=0).astype(jnp.int32)


def draw_degree(key, part):
    counts = jax.random.randint(jax.random.fold_in(key, 21), (FRAMES,), 2, DEG + 1)
    fullest = jax.random.randint(jax.random.fold_in(key, 22), (), 0, FRAMES)
    frame_ids = jnp.arange(FRAMES, dtype=jnp.int32)
    return jnp.where(frame_ids == fullest, DEG, counts).astype(jnp.int32)


def levels(own_key, extent, cuts, low, top_value):
    def one(dim, parts):
        heights = jax.random.uniform(jax.random.fold_in(jax.random.fold_in(own_key, 6), dim), (parts,), jnp.float32, low / len(cuts), top_value / len(cuts))
        return jnp.repeat(jnp.exp(heights), extent[dim] // parts).reshape((-1,) + (1,) * (len(extent) - dim - 1))

    factor_of = one(*cuts[0])
    for cut in cuts[1:]:
        factor_of = factor_of * one(*cut)
    return factor_of


def normal_values(own_key, shape, deviation, limit, split=(), kind=jnp.bfloat16):
    drawn = jax.random.normal(own_key, shape, jnp.float32) * deviation
    if len(split) > 0:
        drawn = levels(own_key, shape, split, -0.22, 0.18) * drawn
    return jnp.clip(drawn, min=-limit, max=limit).astype(kind)


def setup_inputs(seed: int = 0) -> dict:
    streams_of = jax.random.split(jax.random.key(seed), 9)
    return {
        "inv_depth": jnp.clip(0.3 + 1.7 * jax.random.uniform(streams_of[0], (FRAMES, PIXELS), jnp.float32) ** levels(streams_of[0], (FRAMES, PIXELS), ((0, 64),), -0.2, 0.2), 0.3, 2.0),
        "poses": normal_values(streams_of[1], (6, FRAMES), 0.2, 1.2, ((1, 64),), jnp.float32),
        "targets": draw_targets(jax.random.fold_in(streams_of[8], 71), 0),
        "degree": draw_degree(jax.random.fold_in(streams_of[8], 71), 0),
        "flow": normal_values(streams_of[4], (FRAMES, DEG, 2, PIXELS), 1.0, 6.0, ((0, 64), (1, 8))),
        "confidence": jnp.clip(jnp.exp(math.log(1.0) - 2.306499 * jax.random.uniform(streams_of[5], (FRAMES, DEG, PIXELS), jnp.float32) ** levels(streams_of[5], (FRAMES, DEG, PIXELS), ((0, 64), (1, 8)), -0.2, 0.2)), 0.099609375, 1.0).astype(jnp.bfloat16),
        "damping_index": jax.random.randint(streams_of[6], (1,), 4096, 4160).astype(jnp.int32),
        "panel_index": jax.random.randint(streams_of[7], (1,), 0, FRAMES // PANEL_F).astype(jnp.int32),
    }


PRECISE = lax.Precision.HIGHEST

def pixel_grid(pixels):
    pixel_index = jnp.arange(pixels, dtype=jnp.int32)
    pixel_column = (pixel_index % COLS).astype(jnp.float32)
    pixel_row = (pixel_index // COLS).astype(jnp.float32)
    image_rows = pixels // COLS
    horizontal = (pixel_column - 0.5 * (COLS - 1)) / (0.5 * COLS)
    vertical = (pixel_row - 0.5 * (image_rows - 1)) / (0.5 * COLS)
    return (horizontal, vertical)

def damping_value(damping_index):
    level = (damping_index[0] - 4096).astype(jnp.float32)
    return 0.3 * jnp.exp(0.05 * level)

def edge_terms(motion, inv_depth, flow, confidence, live_mask, horizontal, vertical, factor):
    depth_full = jnp.broadcast_to(inv_depth, confidence.shape)
    across = jnp.broadcast_to(horizontal, confidence.shape)
    upward = jnp.broadcast_to(vertical, confidence.shape)
    nothing = jnp.zeros_like(depth_full)
    horiz_jacobian = jnp.stack([-depth_full, nothing, across * depth_full, across * upward, -(1.0 + across * across), upward], axis=2)
    vert_jacobian = jnp.stack([nothing, -depth_full, upward * depth_full, 1.0 + upward * upward, -across * upward, -across], axis=2)
    horiz_pred = jnp.sum(horiz_jacobian * motion[:, :, :, None], axis=2)
    vert_pred = jnp.sum(vert_jacobian * motion[:, :, :, None], axis=2)
    flow_float = flow.astype(jnp.float32)
    horiz_resid = flow_float[:, :, 0, :] - horiz_pred
    vert_resid = flow_float[:, :, 1, :] - vert_pred
    horiz_slope = motion[:, :, 2:3] * across - motion[:, :, 0:1]
    vert_slope = motion[:, :, 2:3] * upward - motion[:, :, 1:2]
    weight = confidence.astype(jnp.float32) * live_mask[:, :, None] * factor
    hessian = jnp.einsum('fskp,fslp->fskl', horiz_jacobian * weight[:, :, None, :], horiz_jacobian, precision=PRECISE)
    hessian = hessian + jnp.einsum('fskp,fslp->fskl', vert_jacobian * weight[:, :, None, :], vert_jacobian, precision=PRECISE)
    gradient = jnp.sum((horiz_jacobian * horiz_resid[:, :, None, :] + vert_jacobian * vert_resid[:, :, None, :]) * weight[:, :, None, :], axis=3)
    cross = (horiz_jacobian * horiz_slope[:, :, None, :] + vert_jacobian * vert_slope[:, :, None, :]) * weight[:, :, None, :]
    curvature = weight * (horiz_slope * horiz_slope + vert_slope * vert_slope)
    depth_grad = weight * (horiz_slope * horiz_resid + vert_slope * vert_resid)
    return (hessian, gradient, cross, curvature, depth_grad)

def panel_columns(targets, own_frames, panel_first, panel_width):
    components = jnp.arange(6, dtype=jnp.int32)
    places = jnp.arange(panel_width, dtype=jnp.int32)
    target_cols = (targets[:, :, None] - panel_first) * 6 + components
    own_cols = (own_frames[:, None] - panel_first) * 6 + components
    mapping = (target_cols[:, :, :, None] == places).astype(jnp.float32)
    return mapping - (own_cols[:, None, :, None] == places).astype(jnp.float32)

def assemble(row_blocks, reduced_grad, slot_targets, own_frames, total_rows):
    components = jnp.arange(6, dtype=jnp.int32)
    target_rows = (slot_targets[:, :, None] * 6 + components).reshape(-1)
    own_rows = (own_frames[:, None] * 6 + components).reshape(-1)
    panel_width = row_blocks.shape[-1]
    column = jnp.zeros((total_rows, panel_width), jnp.float32)
    column = column.at[target_rows].add(row_blocks.reshape(-1, panel_width))
    column = column.at[own_rows].add(-jnp.sum(row_blocks, axis=1).reshape(-1, panel_width))
    right_side = jnp.zeros((total_rows,), jnp.float32)
    right_side = right_side.at[target_rows].add(reduced_grad.reshape(-1))
    right_side = right_side.at[own_rows].add(-jnp.sum(reduced_grad, axis=1).reshape(-1))
    return (column, right_side)

def finish(corner, corner_rhs, block_rows, block_rhs):
    chol_lower = jnp.linalg.cholesky(corner)
    panel = jax.scipy.linalg.solve_triangular(chol_lower, block_rows.T, lower=True).T
    solved = jax.scipy.linalg.solve_triangular(chol_lower, corner_rhs, lower=True)
    updated = block_rhs - jnp.dot(panel, solved, precision=PRECISE)
    return (panel, updated)

def reference(inv_depth, poses, targets, degree, flow, confidence, damping_index, panel_index):
    frames, pixels = inv_depth.shape
    slot_count = targets.shape[1]
    factor = 4.0 / pixels
    damping = damping_value(damping_index)
    horizontal, vertical = pixel_grid(pixels)
    live_mask = (jnp.arange(slot_count, dtype=jnp.int32)[None, :] < degree[:, None]).astype(jnp.float32)
    frame_ids = jnp.arange(frames, dtype=jnp.int32)
    motion = jnp.transpose(jnp.take(poses, targets, axis=1), (1, 2, 0)) - poses.T[:, None, :]
    panel_first = panel_index[0] * PANEL_F
    panel_width = 6 * PANEL_F
    mapping = panel_columns(targets, frame_ids, panel_first, panel_width)

    def block_terms(block):
        block_motion, block_depth, block_flow, block_conf, block_live, block_map = block
        hessian, gradient, cross, curvature, depth_grad = edge_terms(block_motion, block_depth[:, None, :], block_flow, block_conf, block_live, horizontal, vertical, factor)
        damped = (1.0 + damping) * jnp.sum(curvature, axis=1) + 0.05 * damping * factor
        inverse = 1.0 / damped
        weighted = inverse * jnp.sum(depth_grad, axis=1)
        cross_hat = lax.optimization_barrier(cross.astype(jnp.bfloat16)).astype(jnp.float32)
        schur = jnp.einsum('fakp,fblp->fakbl', cross_hat * inverse[:, None, None, :], cross_hat, precision=PRECISE)
        reduce_term = jnp.einsum('fakp,fp->fak', cross_hat, weighted, precision=PRECISE)
        identity = jnp.eye(slot_count, dtype=jnp.float32)
        diag_part = identity[None, :, None, :, None] * hessian[:, :, :, None, :]
        row_blocks = jnp.einsum('fakbl,fblc->fakc', diag_part - schur, block_map, precision=PRECISE)
        return (row_blocks, gradient - reduce_term)

    def by_blocks(source):
        return source.reshape((N_FRAME, frames // N_FRAME) + source.shape[1:])
    row_blocks, reduced_grad = lax.map(block_terms, (by_blocks(motion), by_blocks(inv_depth), by_blocks(flow), by_blocks(confidence), by_blocks(live_mask), by_blocks(mapping)))
    row_blocks = row_blocks.reshape((frames,) + row_blocks.shape[2:])
    reduced_grad = reduced_grad.reshape((frames,) + reduced_grad.shape[2:])
    column, right_side = assemble(row_blocks, reduced_grad, targets, frame_ids, 6 * frames)
    diag_cols = jnp.arange(panel_width, dtype=jnp.int32)
    column = column.at[panel_first * 6 + diag_cols, diag_cols].add(damping)
    corner = lax.dynamic_slice_in_dim(column, panel_first * 6, panel_width, 0)
    corner_rhs = lax.dynamic_slice_in_dim(right_side, panel_first * 6, panel_width, 0)
    return finish(corner, corner_rhs, column, right_side)
```

```python
import numpy as np
import jax
import jax.numpy as jnp
from jax import lax
from jax.experimental import pallas as pl
from jax.experimental.pallas import tpu as pltpu
from jax.sharding import PartitionSpec as P

COLS = 80
PANEL_F = 8
PIXELS = 1280
SLOTS = 8
OWN = 4
FACTOR = 4.0 / PIXELS
PITCH = 42
STEP = 8
INTERPRET = False
F32 = jnp.float32
BF16 = jnp.bfloat16
HIGH = lax.Precision.HIGHEST

VMEM = pl.BlockSpec(memory_space=pltpu.VMEM)
SMEM = pl.BlockSpec(memory_space=pltpu.SMEM)


def basis_rows():
    p = np.arange(PIXELS)
    x = ((p % COLS).astype(np.float32) - np.float32(0.5 * (COLS - 1))) / np.float32(0.5 * COLS)
    rows = PIXELS // COLS
    y = ((p // COLS).astype(np.float32) - np.float32(0.5 * (rows - 1))) / np.float32(0.5 * COLS)
    x = x.astype(np.float64)
    y = y.astype(np.float64)
    r2 = x * x + y * y
    out = np.zeros((16, PIXELS))
    out[:12] = [
        np.ones(PIXELS), x, y, r2, x * y, 1 + x * x, 1 + y * y, y * (1 + r2), x * (1 + r2),
        x * x * y * y + (1 + y * y) ** 2, x * y * (2 + r2), (1 + x * x) ** 2 + x * x * y * y,
    ]
    return out.astype(np.float32)


def moment_map():
    one, x, y, r2, xy, xx1, yy1, yr, xr, h44, h45, h55 = range(12)
    m = np.zeros((128, 128), np.float32)

    def hess(block, row, k, l, sign):
        m[16 * block + row, 6 * k + l] = sign
        m[16 * block + row, 6 * l + k] = sign

    for row, k, l, sign in [(one, 0, 0, 1), (one, 1, 1, 1), (x, 0, 2, -1), (y, 1, 2, -1), (r2, 2, 2, 1)]:
        hess(0, row, k, l, sign)
    for row, k, l, sign in [(xy, 0, 3, -1), (xx1, 0, 4, 1), (y, 0, 5, -1), (yy1, 1, 3, -1), (xy, 1, 4, 1),
                            (x, 1, 5, 1), (yr, 2, 3, 1), (xr, 2, 4, -1)]:
        hess(1, row, k, l, sign)
    for row, k, l, sign in [(h44, 3, 3, 1), (h45, 3, 4, -1), (x, 3, 5, -1), (h55, 4, 4, 1), (y, 4, 5, -1),
                            (r2, 5, 5, 1)]:
        hess(2, row, k, l, sign)
    for block, row, c, sign in [(3, one, 0, -1), (4, one, 1, -1), (3, x, 2, 1), (4, y, 2, 1), (5, xy, 3, 1),
                                (6, yy1, 3, 1), (5, xx1, 4, -1), (6, xy, 4, -1), (5, y, 5, 1), (6, x, 5, -1)]:
        m[16 * block + row, 64 + c] = sign
    return m


def slot_map():
    m = np.zeros((384, 1024), np.float32)
    for k in range(6):
        for l in range(6):
            for b in range(8):
                m[64 * k + 8 * l + b, 128 * b + 6 * k + l] = 1
        m[64 * k + 48, 64 + k] = 1
    return m


def rank_map():
    return np.triu(np.ones((256, 256), np.float32), 1)


def column_map():
    m = np.zeros((3, 128, 384), np.float32)
    for g in range(3):
        for q in range(8):
            for l in range(6):
                for k in range(6):
                    m[g, PITCH * g + 6 * k + l, 48 * k + 6 * q + l] = 1
                m[g, PITCH * g + 37 + l % 3, 288 + 6 * q + l] = 1
    return m


def row_map():
    m = np.zeros((80, 112), np.float32)
    for k in range(6):
        for q in range(8):
            m[6 * q + k, 16 * k + q] = 1
        for r in range(4):
            m[48 + 6 * r + k, 16 * k + 8 + r] = 1
    m[72, 16 * 6 + 12:16 * 6 + 14] = 1
    return m


def lane_codes():
    m = -np.ones((8, 384), np.float32)
    for k in range(7):
        for q in range(8):
            for l in range(6):
                m[0, 48 * k + 6 * q + l] = q
                if k == 6:
                    m[1, 48 * k + 6 * q + l] = l // 3
    return m


def iota(shape, dim, dtype=jnp.int32):
    out = lax.broadcasted_iota(jnp.int32, shape, dim)
    return out if dtype == jnp.int32 else out.astype(dtype)


def thirds(x):
    a = x.astype(BF16)
    r = x - a.astype(F32)
    b = r.astype(BF16)
    return a, b, (r - b.astype(F32)).astype(BF16)


def dot(a, b):
    return lax.dot_general(a, b, (((1,), (0,)), ((), ())), preferred_element_type=F32)


def dot_lanes(a, b, precision=None):
    return lax.dot_general(a, b, (((1,), (1,)), ((), ())), precision=precision, preferred_element_type=F32)


def damping_of(didx_ref):
    level = (didx_ref[0] - 4096).astype(F32)
    return 0.3 * jnp.exp(0.05 * jnp.full((8, 128), level, F32))[0:1, 0:1]


def edge_kernel(ids, pidx, didx, degree, g_ref, d_ref, inv_ref, basis_ref, mmap_ref, smap_ref, rank_ref,
                out_ref, raw_ref, scl_ref, gram_ref, mom_ref, bst_ref):
    e = ids[0]
    f = ids[1]
    pf = pidx[0] * PANEL_F
    pff = pf.astype(F32)
    lane = iota((8, 128), 1)
    sub = iota((8, 128), 0)
    damping = damping_of(didx)

    names = jnp.concatenate([g_ref[pl.ds(0, 64, 4), :], g_ref[pl.ds(1, 64, 4), :]], axis=1)
    frame_row = iota((64, 256), 0)
    here = jnp.sum(jnp.where(frame_row == f, names, 0.0), axis=0, keepdims=True)
    local = names - pff
    earlier = jnp.where(frame_row < f, local, -1.0)
    named = jnp.where(here - pff == iota((8, 256), 0, F32), 1.0, 0.0)
    counts = jnp.concatenate(
        [jnp.sum(jnp.where(earlier == float(q), 1.0, 0.0), axis=0, keepdims=True) for q in range(8)], axis=0)
    rank = dot(named, rank_ref[...]) + jnp.sum(counts, axis=1, keepdims=True)
    slots = jnp.sum(named * (8.0 * iota((8, 256), 0, F32) + rank + 1.0), axis=0, keepdims=True) - 1.0
    row256 = iota((256, 256), 0)
    col256 = iota((256, 256), 1)
    pick = ((row256 & 31) == e * OWN + ((col256 >> 3) & 3)) & ((row256 >> 5) == (col256 >> 5))
    slots = dot(jnp.broadcast_to(slots, (8, 256)), pick.astype(F32))[0:1]
    slots = slots.astype(jnp.int32)
    lane256 = iota((1, 256), 1)
    lane128 = iota((1, 128), 1)
    own_q = f * 32 + e * OWN + (lane128 >> 3) - pf
    own_ok = (lane128 < 32) & (own_q >= 0) & (own_q < 8)

    lane256s = iota((8, 256), 1)
    tcols = [jnp.sum(jnp.where(lane256s == iota((8, 256), 0) * 32 + (e * OWN + i), here, 0.0), axis=1, keepdims=True)
             for i in range(OWN)]
    tcol = jnp.concatenate(tcols, axis=0)
    ocol = (f * 32 + e * OWN + (iota((32, 1), 0) >> 3)).astype(F32)
    both = jnp.concatenate([tcol, ocol], axis=0)
    chunk = jnp.floor(both * (1.0 / 32.0))
    within = both - 32.0 * chunk
    hot = (iota((64, 64), 1, F32) == chunk).astype(F32).astype(BF16)
    poses = jnp.concatenate([g_ref[pl.ds(2, 64, 4), :], g_ref[pl.ds(3, 64, 4), :]], axis=1)
    poses = sum(dot(hot, part) for part in thirds(poses))
    lane64 = iota((64, 256), 1, F32)
    motions = []
    for c in range(6):
        val = jnp.sum(jnp.where(lane64 == 32.0 * c + within, poses, 0.0), axis=1, keepdims=True)
        motions.append(val[0:32] - val[32:64])

    x = basis_ref[1:2, :]
    y = basis_ref[2:3, :]
    xy = basis_ref[4:5, :]
    xx1 = basis_ref[5:6, :]
    yy1 = basis_ref[6:7, :]
    basis = basis_ref[...]
    scl_ref[56:64, :] = jnp.zeros((8, PIXELS), F32)
    mom_ref[...] = jnp.zeros((32, 128), F32)
    for i in range(OWN):
        t1, t2, t3, w1, w2, w3 = [m[8 * i:8 * i + 8] for m in motions]
        d = inv_ref[pl.ds(e * OWN + i, 1), :]
        live = jnp.where(iota((8, 1), 0) < degree[e * OWN + i], 1.0, 0.0)
        weight = d_ref[3 * i + 2] * (live * FACTOR)
        sh = t3 * x - t1
        sv = t3 * y - t2
        rh = d_ref[3 * i] - (d * sh + xy * w1 - xx1 * w2 + y * w3)
        rv = d_ref[3 * i + 1] - (d * sv + yy1 * w1 - xy * w2 - x * w3)
        wsh = weight * sh
        wsv = weight * sv
        curvature = jnp.sum(wsh * sh + wsv * sv, axis=0, keepdims=True)
        slope_grad = jnp.sum(wsh * rh + wsv * rv, axis=0, keepdims=True)
        damped = (1.0 + damping) * curvature + (0.05 * FACTOR) * damping
        inverse = 1.0 / damped
        raw_ref[0:8, :] = -d * wsh
        raw_ref[8:16, :] = -d * wsv
        raw_ref[16:24, :] = d * (x * wsh + y * wsv)
        raw_ref[24:32, :] = xy * wsh + yy1 * wsv
        raw_ref[32:40, :] = -(xx1 * wsh + xy * wsv)
        raw_ref[40:48, :] = y * wsh - x * wsv
        hat = raw_ref[...].astype(BF16)
        scl_ref[0:48, :] = hat.astype(F32) * inverse
        scl_ref[48:56, :] = jnp.broadcast_to(inverse * slope_grad, (8, PIXELS))
        scl = scl_ref[...]
        high = scl.astype(BF16)
        low = (scl - high.astype(F32)).astype(BF16)
        gram = dot_lanes(hat, high) + dot_lanes(hat, low)
        for k in range(6):
            gram_ref[8 * i:8 * i + 8, 64 * k:64 * k + 64] = gram[8 * k:8 * k + 8, :]
        wd = weight * d
        wrh = weight * rh
        wrv = weight * rv
        rows = jnp.concatenate([wd * d, wd, weight, d * wrh, d * wrv, wrh, wrv], axis=0)
        mom = dot_lanes(rows, basis, HIGH)
        for k in range(7):
            mom_ref[8 * i:8 * i + 8, 16 * k:16 * k + 16] = mom[8 * k:8 * k + 8, :]

    hess = sum(dot(part, mmap_ref[...]) for part in thirds(mom_ref[...]))
    gram = sum(dot(part, smap_ref[...]) for part in thirds(gram_ref[...]))
    lane32 = iota((32, 128), 1)
    sub32 = iota((32, 128), 0)
    slot32 = sub32 & 7
    reduced = jnp.where((lane32 >= 64) & (lane32 < 70), hess - gram[:, 0:128], 0.0)
    first = pltpu.roll(reduced, 128 - 27, 1)
    second = pltpu.roll(reduced, 128 - 30, 1)
    ids_block = jnp.where(lane32 == 36, tcol, jnp.where(lane32 == 40, ocol, 0.0))
    own_block = jnp.zeros((32, 128), F32)
    grad_lanes = (lane32 >= 37) & (lane32 < 40)
    for b in range(8):
        block = jnp.where(slot32 == b, hess, 0.0) - gram[:, 128 * b:128 * b + 128]
        block = jnp.where(lane32 < 36, block, 0.0)
        lift = jnp.concatenate(
            [jnp.where(sub == 0, first[8 * i + b:8 * i + b + 1, :], second[8 * i + b:8 * i + b + 1, :])
             for i in range(OWN)], axis=0)
        block = block + jnp.where(grad_lanes & (slot32 < 2), lift, 0.0)
        own_block = own_block - block
        bst_ref[32 * b:32 * b + 32, :] = block + ids_block
    bst_ref[256:288, :] = own_block + ids_block
    bst_ref[288:384, :] = jnp.zeros((96, 128), F32)

    qn = slots >> 3
    jn = slots & 7
    gn = (jn >= 3).astype(jnp.int32) + (jn >= 6).astype(jnp.int32)
    an = lane256 & 7
    row_n = qn * 24 + (jn - 3 * gn) * 8 + an
    row_o = own_q * 24 + 16 + (lane128 & 7)
    stack = bst_ref[...]
    rows192 = iota((192, 384), 0)
    records = jnp.zeros((192, 128), F32)
    for g in range(3):
        naming = jnp.where((slots >= 0) & (gn == g), row_n, -1)
        owning = jnp.where(own_ok, row_o, -1) if g == 2 else jnp.full((1, 128), -1, jnp.int32)
        code = jnp.concatenate([naming, owning], axis=1)
        choose = (rows192 == code).astype(F32).astype(BF16)
        shifted = pltpu.roll(stack, PITCH * g, 1) if g else stack
        for part in thirds(shifted):
            records = records + dot(choose, part)

    lift8 = (lane == sub + 64).astype(F32)
    rg = dot_lanes(lift8, reduced, HIGH)
    frames = iota((32, 2048), 1).astype(F32)
    spread = ((frames == tcol).astype(F32) - (frames == ocol).astype(F32)).astype(BF16)
    rhs = sum(dot(jnp.concatenate([part.astype(F32), jnp.zeros((8, 32), F32)], axis=0).astype(BF16), spread)[0:8]
              for part in thirds(rg))
    for q in range(8):
        out_ref[q, 0:24, :] = records[24 * q:24 * q + 24, :]
        out_ref[q, 24:32, :] = rhs[:, 256 * q:256 * q + 128]
        out_ref[q, 32:40, :] = rhs[:, 256 * q + 128:256 * q + 256]


def edge_stage(ids, pidx, didx, degree, gathered, data, inv_depth):
    consts = (jnp.asarray(basis_rows()), jnp.asarray(moment_map(), BF16), jnp.asarray(slot_map(), BF16),
              jnp.asarray(rank_map()))
    return pl.pallas_call(
        edge_kernel,
        out_shape=on_chip((8, 40, 128)),
        in_specs=[SMEM] * 4 + [VMEM] * 7,
        out_specs=VMEM,
        scratch_shapes=[
            pltpu.VMEM((48, PIXELS), F32), pltpu.VMEM((64, PIXELS), F32), pltpu.VMEM((32, 384), F32),
            pltpu.VMEM((32, 128), F32),
            pltpu.VMEM((384, 128), F32),
        ],
        name="edge_stage",
        interpret=INTERPRET,
    )(ids, pidx, didx, degree, near(gathered), near(data), near(inv_depth), *[near(c) for c in consts])


def on_chip(shape):
    return jax.ShapeDtypeStruct(shape, F32) if INTERPRET else pltpu.VMEM(shape, F32)


def near(x):
    return x if INTERPRET else pltpu.with_memory_space_constraint(x, pltpu.VMEM)


def total(ref):
    out = ref[0]
    for k in range(1, 8):
        out = out + ref[k]
    return out


def sum_edge_kernel(in_ref, out_ref):
    s = total(in_ref)
    for k in range(8):
        out_ref[k, 0:24, :] = s[0:24]
        out_ref[k, 24:32, :] = s[24 + 8 * (k // 4):32 + 8 * (k // 4)]


def sum_y_kernel(in_ref, out_ref):
    s = total(in_ref)
    for k in range(8):
        out_ref[k] = s


def sum_z_kernel(in_ref, out_ref, rhs_ref):
    s = total(in_ref)
    for k in range(8):
        out_ref[k] = s[0:24]
    rhs_ref[...] = s[24:32]


def small_call(kernel, shapes, name, *args):
    return pl.pallas_call(
        kernel,
        out_shape=[on_chip(s) for s in shapes],
        in_specs=[VMEM] * len(args),
        out_specs=[VMEM] * len(shapes),
        name=name,
        interpret=INTERPRET,
    )(*[near(a) for a in args])


def finish_kernel(ids, pidx, didx, r_ref, rb_ref, cmap_ref, rmap_ref, code_ref, panel_ref, upd_ref, cst_ref):
    e = ids[0]
    f = ids[1]
    pf = pidx[0] * PANEL_F
    own0 = (e * 64 + f) * OWN
    damping = damping_of(didx)
    r = r_ref[...].reshape(192, 128)
    rid = iota((128, 1), 0) & 15
    rho = jnp.where(rid < 8, pf + rid, own0 + rid - 8).astype(F32)
    recs = iota((1, 192), 1)
    half = jnp.where((rid - 12) == (recs & 7), 1.0, 0.0)
    mine = jnp.floor((recs.astype(F32) + 0.5) * (1.0 / 24.0)) == (iota((128, 1), 0) >> 4).astype(F32)
    parts = thirds(r)
    c = jnp.zeros((128, 384), F32)
    idrow = iota((16, 128), 0)
    idlane = jnp.where(idrow < 3, PITCH * idrow + 36, PITCH * (idrow - 3) + 40)
    find = ((iota((16, 128), 1) == idlane) & (idrow < 6)).astype(F32).astype(BF16)
    names = sum(dot_lanes(find, part) for part in parts)
    for g in range(3):
        w = jnp.where(names[g:g + 1] == rho, 1.0, 0.0) - jnp.where(names[g + 3:g + 4] == rho, 1.0, 0.0)
        w = jnp.where(mine, jnp.where(rid < 12, w, half), 0.0).astype(BF16)
        picked = sum(dot(w, part) for part in parts)
        c = c + sum(dot(part, cmap_ref[g]) for part in thirds(picked))
    qlane = code_ref[0:1, :]
    alane = code_ref[1:2, :]
    keep = (qlane == (iota((128, 1), 0) >> 4).astype(F32)) & ((alane < 0.0) | (alane == (rid - 12).astype(F32)))
    c = jnp.sum(jnp.where(keep, c, 0.0).reshape(8, 16, 384), axis=0)
    lane16 = iota((16, 128), 1)
    for k in range(7):
        turned = pltpu.roll(c, 384 - 48 * k, 1) if k else c
        cst_ref[16 * k:16 * k + 16, :] = jnp.where(lane16 < 48, turned[:, 0:128], 0.0)
    a = sum(dot(rmap_ref[...], part) for part in thirds(cst_ref[...]))
    row = iota((80, 128), 0)
    lane = iota((80, 128), 1)
    shift = 6 * (own0 - pf) - 48
    diag = ((row < 48) & (lane == row)) | ((row >= 48) & (row < 72) & (lane == row + shift) & (lane < 48))
    a = a + jnp.where(diag, damping, 0.0)
    lane1 = iota((1, 128), 1)
    dvec = jnp.ones((1, 128), F32)
    for start in range(0, 48, STEP):
        cols = [jnp.broadcast_to(a[:, j:j + 1], a.shape) for j in range(start, start + STEP)]
        for m in range(STEP):
            j = start + m
            pivot = cols[m][m:m + 1, :]
            dvec = jnp.where(lane1 == j, pivot, dvec)
            inverse = 1.0 / pivot
            line = jnp.where(lane1 > j, a[m:m + 1, :] * inverse, 0.0)
            for n in range(m + 1, STEP):
                cols[n] = cols[n] - cols[m] * (cols[n][m:m + 1, :] * inverse)
            a = a - cols[m] * line
        a = a[STEP:]
    scale = 1.0 / jnp.sqrt(dvec)
    a = a * scale
    panel = a[0:24]
    panel_ref[...] = panel[:, 0:48]
    z = a[24:25]
    lane24 = iota((24, 128), 1)
    row24 = iota((24, 128), 0)
    r24 = (row24 >= 6).astype(jnp.int32) + (row24 >= 12).astype(jnp.int32) + (row24 >= 18).astype(jnp.int32)
    first = ((f >> 3) & 3) * 32 + (f & 7) * 4
    rb = rb_ref[...]
    rb24 = jnp.concatenate([rb[0:6], rb[0:6], rb[0:6], rb[0:6]], axis=0)
    mixed = jnp.where(lane24 == first + r24, rb24, 0.0) - panel * z
    upd_ref[...] = dot_lanes(jnp.ones((8, 128), F32), mixed, HIGH)[0:1]


def finish_stage(ids, pidx, didx, records, rhs):
    consts = (jnp.asarray(column_map(), BF16), jnp.asarray(row_map(), BF16), jnp.asarray(lane_codes()))
    return pl.pallas_call(
        finish_kernel,
        out_shape=[jax.ShapeDtypeStruct((24, 48), F32), jax.ShapeDtypeStruct((1, 24), F32)],
        in_specs=[SMEM] * 3 + [VMEM] * 5,
        out_specs=[VMEM, VMEM],
        scratch_shapes=[pltpu.VMEM((112, 128), F32)],
        name="finish_stage",
        interpret=INTERPRET,
    )(ids, pidx, didx, near(records), near(rhs), *[near(c) for c in consts])


def graph_kernel(targets_ref, poses_ref, out_ref):
    rows = [targets_ref[k:k + 1, :].astype(F32) for k in range(8)]
    rows += [poses_ref[k:k + 1, :] for k in range(6)] + [jnp.zeros((1, 32), F32)] * 2
    tile = jnp.concatenate([jnp.concatenate(rows[4 * k:4 * k + 4], axis=1) for k in range(4)] * 2, axis=0)
    out_ref[...] = jnp.broadcast_to(tile[None], (32, 8, 128)).reshape(256, 128)


def graph_message(poses, targets):
    return pl.pallas_call(
        graph_kernel,
        out_shape=on_chip((256, 128)),
        in_specs=[VMEM, VMEM],
        out_specs=VMEM,
        name="graph_message",
        interpret=INTERPRET,
    )(targets.T, poses)


def data_message(flow, confidence):
    frames = flow.shape[0]
    both = jnp.concatenate([flow[:, 0], confidence], axis=1)
    return both.reshape(8, frames // 8 * 3, PIXELS)


def data_layout(received):
    return jnp.transpose(received, (1, 0, 2)).astype(F32)


def per_device(inv_depth, poses, targets, degree, flow, confidence, damping_index, panel_index):
    e = lax.axis_index("edge")
    f = lax.axis_index("frame")
    ids = jnp.stack([e, f]).astype(jnp.int32)
    along_y = [[8 * y + z for y in range(8)] for z in range(8)]
    along_z = [[8 * y + z for z in range(8)] for y in range(8)]

    def exchange(x, axis, groups=None):
        return lax.all_to_all(x, axis, 0, 0, axis_index_groups=groups)

    gathered = exchange(graph_message(poses, targets).reshape(64, 4, 128), "frame")
    gathered, raw = lax.optimization_barrier((gathered, data_message(flow, confidence)))
    gathered = gathered.reshape(256, 128)
    data = data_layout(exchange(raw, "edge"))
    part = edge_stage(ids, panel_index, damping_index, degree, gathered, data, inv_depth)
    part = exchange(part, "edge")
    (part,) = small_call(sum_edge_kernel, [(8, 32, 128)], "sum_edge", part)
    part = exchange(part, "frame", along_y)
    (part,) = small_call(sum_y_kernel, [(8, 32, 128)], "sum_y", part)
    part = exchange(part, "frame", along_z)
    records, rhs = small_call(sum_z_kernel, [(8, 24, 128), (8, 128)], "sum_z", part)
    records = exchange(records, "edge")
    panel, updated = finish_stage(ids, panel_index, damping_index, records, rhs)
    return panel, updated.reshape(24)


def solution(mesh):
    placed = (
        P("frame", None),
        P(None, "frame"),
        P("frame", None),
        P("frame"),
        P("frame", "edge", None, None),
        P("frame", "edge", None),
        P(),
        P(),
    )
    return jax.shard_map(
        per_device,
        mesh=mesh,
        in_specs=placed,
        out_specs=(P(("edge", "frame"), None), P(("edge", "frame"))),
        check_vma=False,
    )
```
